32 devices in a mesh: depth: 4 (over x, core), map: 8 (over z, y).
Axes of the slice: x: 2, y: 2, z: 4, core: 2. Of those that a mesh axis runs over, the one named last changes fastest.
Arguments:
- adjoint: float32 [35, 9, 16384], P(None, None, ('depth', 'map')), may hold values from -6 to 6
- forward: bfloat16 [2, 35, 9, 16384], P(None, None, None, ('depth', 'map')), may hold values from -6 to 6
- p_speed: float32 [16384], P(('depth', 'map')), may hold values from 1.5 to 2.5
- s_speed: float32 [16384], P(('depth', 'map')), may hold values from 0.5 to 1
- density: float32 [16384], P(('depth', 'map')), may hold values from 0.8 to 1.6
- inv_jacobian: float32 [3, 3, 16384], P(None, None, ('depth', 'map')), may hold values from -1 to 1
- face_angles: float32 [2, 4, 16384], P(None, None, ('depth', 'map')), may hold values from -3.140625 to 3.140625
- face_scale: float32 [4, 16384], P(None, ('depth', 'map')), may hold values from 0.25 to 1
- stiffness: float32 [3, 35, 35], replicated, may hold values from -1 to 1
- face_basis: float32 [4, 35, 15], replicated, may hold values from -1 to 1
- neighbours: int32 [4, 16384], P(None, ('depth', 'map')), may hold values from 0 to 768, as said below
- neighbour_face: int32 [4, 16384], P(None, ('depth', 'map')), may hold values from 0 to 3
- send_elements: int32 [4, 2048], P(None, ('depth', 'map')), may hold values from 0 to 511
- send_faces: int32 [4, 2048], P(None, ('depth', 'map')), may hold values from 0 to 3
- cell_index: int32 [16384], P(('depth', 'map')), may hold values from 0 to 511, as said below
Outputs:
- adjoint_out: float32 [35, 9, 16384], P(None, None, ('depth', 'map'))
- kernels: float32 [3, 512], P(None, ('depth', 'map'))
The draws below stay inside these ranges and needn't reach their ends.
Inputs may be any that keep to these rules, and one draw needn't show every extreme that they name: `neighbours`: entries below 512 name a local element of the same device; 512 + r * 64 + k names entry k of ghost slot r; 768 marks a boundary face. `cell_index`: local element k of device d lies in coarse cell s = d * 16 + k // 32 or in one next to it (s - 1 or s + 1, within 0 to 511); coarse cells are owned cyclically, so the entry is (s mod the number of devices) * 16 + s // the number of devices.
All inputs are finite; a program needn't handle non-finite values.
Results may differ from the reference program's by a relative error of at most 0.0003.
Values sent between devices are 32-bit elements; how exact they have to be, the bound alone decides.
A program may use at most 192 MiB of HBM per device.

```python
import math
import jax
import jax.numpy as jnp
from jax import lax

NF = 9
NB = 35
NBF = 15
PICARD = 4
STEPS = 2
E_DEV = 512
GHOST = 64
CELLS_DEV = 16
ELEMENTS = 16384
GHOSTS = 2048
CELLS = 512
N_DEPTH = 4
N_MAP = 8


def draw_neighbours(key, part):
    limit = E_DEV + 4 * GHOST
    values = jax.random.randint(key, (4, ELEMENTS), 0, limit + 1, dtype=jnp.int32)
    face_rows = lax.broadcasted_iota(jnp.int32, (4, ELEMENTS), 0)
    position = lax.broadcasted_iota(jnp.int32, (4, ELEMENTS), 1) % E_DEV
    values = jnp.where((face_rows == 3) & (position == 0), limit, values)
    values = jnp.where((face_rows == 2) & (position == 0), 0, values)
    return values


def draw_cell_index(key, part):
    device_count = ELEMENTS // E_DEV
    element = lax.broadcasted_iota(jnp.int32, (ELEMENTS,), 0)
    owner_device = element // E_DEV
    local = element % E_DEV
    spatial = owner_device * CELLS_DEV + local // 32
    key_move, key_side = jax.random.split(jax.random.fold_in(key, 11))
    moved = jax.random.randint(key_move, (ELEMENTS,), 0, 4, dtype=jnp.int32) == 0
    side = jax.random.randint(key_side, (ELEMENTS,), 0, 2, dtype=jnp.int32) * 2 - 1
    spatial = spatial + jnp.where(moved, side, 0)
    spatial = jnp.clip(spatial, 0, CELLS - 1)
    spatial = jnp.where(element == 0, 0, spatial)
    spatial = jnp.where(element == ELEMENTS - 1, CELLS - 1, spatial)
    return (spatial % device_count * CELLS_DEV + spatial // device_count).astype(jnp.int32)


def place_ends(values, own_key, least, top_value):
    longest = values.shape.index(max(values.shape))
    spots = []
    for shift in (0, 1):
        where = [jax.random.randint(jax.random.fold_in(own_key, axis), (), 0, length) for axis, length in enumerate(values.shape)]
        where[longest] = (where[longest] + shift) % values.shape[longest]
        spots.append(tuple(where))
    return values.at[spots[0]].set(least).at[spots[1]].set(top_value)


def steps_of(own_key, shape, cuts, smallest, largest):
    factor_of, own = 1.0, jax.random.fold_in(own_key, 6)
    for dim, shards_of in cuts:
        heights = jnp.exp(jax.random.uniform(jax.random.fold_in(own, dim), (shards_of,), jnp.float32, smallest / len(cuts), largest / len(cuts)))
        factor_of = factor_of * jnp.repeat(heights, shape[dim] // shards_of).reshape([-1 if axis == dim else 1 for axis in range(len(shape))])
    return factor_of


def scatter_about(key, dims, scale, most, shards=(), kind=jnp.bfloat16):
    factor_of = steps_of(key, dims, shards, -0.22, 0.18) if shards else 1.0
    entries = jax.random.normal(key, dims, jnp.float32) * scale * factor_of
    return jnp.minimum(jnp.maximum(entries, -most), most).astype(kind)


def setup_inputs(seed: int = 0) -> dict:
    streams_of = jax.random.split(jax.random.key(seed), 16)
    adjoint = scatter_about(streams_of[0], (NB, NF, ELEMENTS), 1.0, 6.0, ((2, 32),), jnp.float32)
    forward = scatter_about(streams_of[1], (STEPS, NB, NF, ELEMENTS), 1.0, 6.0, ((3, 32),))
    p_speed = jnp.clip(jnp.exp(math.log(2.5) - 0.51082562 * jax.random.uniform(streams_of[2], (ELEMENTS,), jnp.float32) ** steps_of(streams_of[2], (ELEMENTS,), ((0, 32),), -0.2, 0.2)), 1.5, 2.5)
    s_speed = jnp.clip(jnp.exp(math.log(1.0) - 0.6931472 * jax.random.uniform(streams_of[3], (ELEMENTS,), jnp.float32) ** steps_of(streams_of[3], (ELEMENTS,), ((0, 32),), -0.2, 0.2)), 0.5, 1.0)
    density = jnp.clip(jnp.exp(math.log(1.6) - 0.6931472 * jax.random.uniform(streams_of[4], (ELEMENTS,), jnp.float32) ** steps_of(streams_of[4], (ELEMENTS,), ((0, 32),), -0.2, 0.2)), 0.8, 1.6)
    inv_jacobian = jnp.clip(jax.random.uniform(streams_of[5], (3, 3, ELEMENTS), jnp.float32, -1.0, 1.0) * steps_of(streams_of[5], (3, 3, ELEMENTS), ((2, 32),), -0.4, 0.0), -1.0, 1.0)
    face_angles = jnp.clip(jax.random.uniform(streams_of[6], (2, 4, ELEMENTS), jnp.float32, -3.140625, 3.140625), -3.140625, 3.140625)
    face_scale = jnp.clip(jnp.exp(math.log(1.0) - 1.3862944 * jax.random.uniform(streams_of[7], (4, ELEMENTS), jnp.float32) ** steps_of(streams_of[7], (4, ELEMENTS), ((1, 32),), -0.2, 0.2)), 0.25, 1.0)
    stiffness = scatter_about(streams_of[8], (3, NB, NB), NB ** -0.5, 1.0, (), jnp.float32)
    face_basis = scatter_about(streams_of[9], (4, NB, NBF), NB ** -0.5, 1.0, (), jnp.float32)
    neighbours = draw_neighbours(jax.random.fold_in(streams_of[15], 71), 0)
    neighbour_face = place_ends(jax.random.randint(streams_of[11], (4, ELEMENTS), 0, 4), jax.random.fold_in(streams_of[11], 1), 0, 3).astype(jnp.int32)
    send_elements = place_ends(jax.random.randint(streams_of[12], (4, GHOSTS), 0, E_DEV), jax.random.fold_in(streams_of[12], 1), 0, E_DEV - 1).astype(jnp.int32)
    send_faces = place_ends(jax.random.randint(streams_of[13], (4, GHOSTS), 0, 4), jax.random.fold_in(streams_of[13], 1), 0, 3).astype(jnp.int32)
    cell_index = draw_cell_index(jax.random.fold_in(streams_of[15], 71), 0)
    return dict(adjoint=adjoint, forward=forward, p_speed=p_speed, s_speed=s_speed, density=density, inv_jacobian=inv_jacobian, face_angles=face_angles, face_scale=face_scale, stiffness=stiffness, face_basis=face_basis, neighbours=neighbours, neighbour_face=neighbour_face, send_elements=send_elements, send_faces=send_faces, cell_index=cell_index)


HIGH = lax.Precision.HIGHEST
TIME_STEP = 0.3
KERNEL_WEIGHT = 0.125


def star_apply(normal, coeffs, field):
    lame_first, shear_mod, inverse_density = coeffs
    along_x, along_y, along_z = normal[0], normal[1], normal[2]
    long_mod = lame_first + 2.0 * shear_mod
    velocity_x, velocity_y, velocity_z = field[:, 6], field[:, 7], field[:, 8]
    rows = [
        -(long_mod * along_x * velocity_x + lame_first * along_y * velocity_y + lame_first * along_z * velocity_z),
        -(lame_first * along_x * velocity_x + long_mod * along_y * velocity_y + lame_first * along_z * velocity_z),
        -(lame_first * along_x * velocity_x + lame_first * along_y * velocity_y + long_mod * along_z * velocity_z),
        -shear_mod * (along_y * velocity_x + along_x * velocity_y),
        -shear_mod * (along_z * velocity_y + along_y * velocity_z),
        -shear_mod * (along_z * velocity_x + along_x * velocity_z),
        -inverse_density * (along_x * field[:, 0] + along_y * field[:, 3] + along_z * field[:, 5]),
        -inverse_density * (along_x * field[:, 3] + along_y * field[:, 1] + along_z * field[:, 4]),
        -inverse_density * (along_x * field[:, 5] + along_y * field[:, 4] + along_z * field[:, 2]),
    ]
    return jnp.stack(rows, axis=1)


def material(p_speed, s_speed, density):
    lame_first = density * (p_speed * p_speed - 2.0 * s_speed * s_speed)
    shear_mod = density * s_speed * s_speed
    return (lame_first, shear_mod, 1.0 / density)


def normal_vectors(face_angles):
    azimuth, polar = face_angles[0], face_angles[1]
    return jnp.stack([jnp.cos(azimuth) * jnp.sin(polar), jnp.sin(azimuth) * jnp.sin(polar), jnp.cos(polar)], axis=0)


def volume_term(dofs, inv_jacobian, coeffs, stiffness):
    basis, fields, count = dofs.shape
    flat = dofs.reshape(basis, fields * count)
    total = jnp.zeros(dofs.shape, jnp.float32)
    for coord in range(3):
        moved = jnp.dot(stiffness[coord].T, flat, precision=HIGH).reshape(basis, fields, count)
        total = total + star_apply(inv_jacobian[coord], coeffs, moved)
    return total


def predict(dofs, inv_jacobian, coeffs, stiffness):
    current = dofs
    for sweep in range(PICARD):
        current = dofs + (0.5 * TIME_STEP) * volume_term(current, inv_jacobian, coeffs, stiffness)
    return TIME_STEP * current


def face_traces(table, face_basis):
    basis, fields, width = table.shape
    face_count, basis_again, modes = face_basis.shape
    columns = jnp.transpose(face_basis, (1, 0, 2)).reshape(basis, face_count * modes)
    projected = jnp.dot(columns.T, table.reshape(basis, fields * width), precision=HIGH)
    return projected.reshape(face_count, modes, fields, width)


def flatten_faces(projected):
    face_count, modes, fields, width = projected.shape
    return jnp.transpose(projected, (1, 2, 0, 3)).reshape(modes, fields, face_count * width)


def apply_faces(update, traces, flat_index, inside, own_width, coeffs, p_speed, normals, face_scale, face_basis):
    basis, fields, count = update.shape
    modes = face_basis.shape[2]
    for face in range(4):
        own = traces[:, :, face * own_width: face * own_width + count]
        far = jnp.take(traces, flat_index[face], axis=2) * inside[face].astype(jnp.float32)
        flux = 0.5 * star_apply(normals[:, face], coeffs, own + far) + (0.5 * p_speed) * (own - far)
        flux = flux * face_scale[face]
        lifted = jnp.dot(face_basis[face], flux.reshape(modes, fields * count), precision=HIGH)
        update = update - lifted.reshape(basis, fields, count)
    return update


def correct(state, integ, ghosts, ghost_faces, coeffs, p_speed, inv_jacobian, normals, face_scale, neighbours, neighbour_face, stiffness, face_basis):
    count = integ.shape[2]
    table = jnp.concatenate([integ, ghosts], axis=2)
    width = table.shape[2]
    traces = flatten_faces(face_traces(table, face_basis))
    inside = neighbours < width
    safe = jnp.minimum(neighbours, width - 1)
    ghost_slot = jnp.clip(safe - count, 0, ghost_faces.shape[0] - 1)
    far_face = jnp.where(safe < count, neighbour_face, ghost_faces[ghost_slot])
    flat_index = (far_face * width + safe).astype(jnp.int32)
    update = state + volume_term(integ, inv_jacobian, coeffs, stiffness)
    return apply_faces(update, traces, flat_index, inside, width, coeffs, p_speed, normals, face_scale, face_basis)


def element_kernels(integ, snapshot, p_speed, s_speed, density):
    forward_field = snapshot.astype(jnp.float32)
    product = integ * forward_field
    trace_adjoint = integ[:, 0] + integ[:, 1] + integ[:, 2]
    trace_forward = forward_field[:, 0] + forward_field[:, 1] + forward_field[:, 2]
    first = jnp.sum(trace_adjoint * trace_forward, axis=0)
    second = jnp.sum(product[:, 0] + product[:, 1] + product[:, 2] + 2.0 * (product[:, 3] + product[:, 4] + product[:, 5]), axis=0)
    third = jnp.sum(product[:, 6] + product[:, 7] + product[:, 8], axis=0)
    speed_kernel = 2.0 * density * p_speed * first
    shear_kernel = density * s_speed * (2.0 * second - 4.0 * first)
    mass_kernel = (p_speed * p_speed - 2.0 * s_speed * s_speed) * first + s_speed * s_speed * second + third
    return KERNEL_WEIGHT * jnp.stack([speed_kernel, shear_kernel, mass_kernel], axis=1)


def to_devices(array):
    count = N_DEPTH * N_MAP
    lead = array.shape[:-1]
    return jnp.moveaxis(array.reshape(lead + (count, array.shape[-1] // count)), -2, 0)


def from_devices(array):
    moved = jnp.moveaxis(array, 0, -2)
    return moved.reshape(moved.shape[:-2] + (moved.shape[-2] * moved.shape[-1],))


def receive(blocks):
    grid = blocks.reshape((N_DEPTH, N_MAP) + blocks.shape[1:])
    zero_depth = jnp.zeros_like(grid[:1, :, 0])
    from_below = jnp.concatenate([zero_depth, grid[:-1, :, 0]], axis=0)
    from_above = jnp.concatenate([grid[1:, :, 1], zero_depth], axis=0)
    zero_map = jnp.zeros_like(grid[:, :1, 2])
    from_left = jnp.concatenate([zero_map, grid[:, :-1, 2]], axis=1)
    from_right = jnp.concatenate([grid[:, 1:, 3], zero_map], axis=1)
    joined = jnp.stack([from_below, from_above, from_left, from_right], axis=2)
    return joined.reshape((N_DEPTH * N_MAP,) + joined.shape[2:])


def reference(adjoint, forward, p_speed, s_speed, density, inv_jacobian, face_angles, face_scale, stiffness, face_basis, neighbours, neighbour_face, send_elements, send_faces, cell_index):
    device_count = N_DEPTH * N_MAP
    state = to_devices(adjoint)
    snaps = to_devices(forward)
    speeds_p = to_devices(p_speed)
    speeds_s = to_devices(s_speed)
    masses = to_devices(density)
    jacobians = to_devices(inv_jacobian)
    normals_all = to_devices(normal_vectors(face_angles))
    scales = to_devices(face_scale)
    nbr = to_devices(neighbours)
    nbr_face = to_devices(neighbour_face)
    sends = to_devices(send_elements)
    ghost_faces = receive(to_devices(send_faces)).reshape(device_count, -1)
    kernels = jnp.zeros((3, CELLS), jnp.float32)

    def predict_item(item):
        return predict(item[0], item[1], material(item[2], item[3], item[4]), stiffness)

    def pick_item(item):
        return jnp.stack([jnp.take(item[0], item[1][slot], axis=2) for slot in range(4)], axis=0)

    def correct_item(item):
        coeffs = material(item[4], item[5], item[6])
        return correct(item[0], item[1], item[2], item[3], coeffs, item[4], item[7], item[8], item[9], item[10], item[11], stiffness, face_basis)

    def kernel_item(item):
        return element_kernels(item[0], item[1], item[2], item[3], item[4])

    for step in range(STEPS):
        integ = lax.map(predict_item, (state, jacobians, speeds_p, speeds_s, masses))
        blocks = lax.map(pick_item, (integ, sends))
        arrived = receive(blocks)
        ghosts = jnp.moveaxis(arrived, 1, -2)
        ghosts = ghosts.reshape(ghosts.shape[:-2] + (ghosts.shape[-2] * ghosts.shape[-1],))
        state = lax.map(correct_item, (state, integ, ghosts, ghost_faces, speeds_p, speeds_s, masses, jacobians, normals_all, scales, nbr, nbr_face))
        terms = lax.map(kernel_item, (integ, snaps[:, step], speeds_p, speeds_s, masses))
        kernels = kernels + jax.ops.segment_sum(terms.reshape(-1, 3), cell_index, num_segments=CELLS).T
    return from_devices(state), kernels
```

```python
import functools

import jax
import jax.numpy as jnp
from jax import lax
from jax.experimental import pallas as pl
from jax.experimental.pallas import tpu as pltpu
from jax.sharding import PartitionSpec as P

MESH = pl.DeviceIdType.MESH
PICARD = 4
HALF = 0.15
FULL = 0.3
KERNEL_WEIGHT = 0.125
F32 = jnp.float32
BF16 = jnp.bfloat16
ROWS = 40
KROWS = 48
TRACE = 144


def split(value):
    high = value.astype(BF16)
    low = (value - high.astype(F32)).astype(BF16)
    return high, low


def wide_dot(left, right):
    return jnp.dot(left, right, preferred_element_type=F32)


def kernel(
    n_depth,
    n_map,
    adj_ref,
    fwd_ref,
    p_ref,
    s_ref,
    rho_ref,
    jac_ref,
    ang_ref,
    scale_ref,
    amat_ref,
    lmat_ref,
    nbr_ref,
    nface_ref,
    send_ref,
    cell_ref,
    out_ref,
    hist_ref,
    q_buf,
    p_buf,
    b_buf,
    y_buf,
    f_buf,
    coef,
    onehot,
    send_hot,
    left_buf,
    ghost_left,
    far_buf,
    flux_buf,
    fx_buf,
    sums,
    send_buf,
    recv_buf,
    cells_out,
    cells_main,
    cells_side,
    g_send,
    g_recv,
    h_send,
    h_recv_main,
    h_recv_side,
):
    n_dev = n_depth * n_map
    count = adj_ref.shape[2]
    basis = adj_ref.shape[1]
    steps = fwd_ref.shape[0]
    tiles = count // 128
    per_dev = count // 32
    total_cells = per_dev * n_dev
    own_i = lax.axis_index("depth")
    own_j = lax.axis_index("map")
    me = own_i * n_map + own_j

    def place(linear):
        return (lax.div(linear, n_map), lax.rem(linear, n_map))

    links = [
        (0, 0, own_i < n_depth - 1, (own_i + 1, own_j), own_i > 0, (own_i - 1, own_j)),
        (1, 0, own_i > 0, (own_i - 1, own_j), own_i < n_depth - 1, (own_i + 1, own_j)),
        (2, 1, own_j < n_map - 1, (own_i, own_j + 1), own_j > 0, (own_i, own_j - 1)),
        (3, 1, own_j > 0, (own_i, own_j - 1), own_j < n_map - 1, (own_i, own_j + 1)),
    ]

    recv_buf[...] = jnp.zeros_like(recv_buf)
    cells_main[...] = jnp.zeros_like(cells_main)
    cells_side[...] = jnp.zeros_like(cells_side)

    barrier = pltpu.get_barrier_semaphore()
    for slot, tile, to_ok, target, from_ok, source in links:

        @pl.when(from_ok)
        def _(source=source):
            pl.semaphore_signal(barrier, inc=1, device_id=source, device_id_type=MESH)

    def main_source(j):
        return lax.div(me + n_dev * j, per_dev)

    def side_source(j):
        cell = me + n_dev * j
        place_in = lax.rem(cell, per_dev)
        home = lax.div(cell, per_dev)
        below = jnp.logical_and(place_in == 0, home > 0)
        above = jnp.logical_and(place_in == per_dev - 1, home < n_dev - 1)
        source = jnp.where(below, home - 1, home + 1)
        return jnp.logical_or(below, above), jnp.clip(source, 0, n_dev - 1)

    def greet(j, carry):
        main = main_source(j)

        @pl.when(main != me)
        def _():
            pl.semaphore_signal(barrier, inc=1, device_id=place(main), device_id_type=MESH)

        exists, side = side_source(j)

        @pl.when(jnp.logical_and(exists, side != me))
        def _():
            pl.semaphore_signal(barrier, inc=1, device_id=place(side), device_id_type=MESH)

        return carry

    lax.fori_loop(0, per_dev, greet, 0)

    p_speed, s_speed, density = p_ref[...], s_ref[...], rho_ref[...]
    lame = density * (p_speed * p_speed - 2.0 * s_speed * s_speed)
    shear = density * s_speed * s_speed
    inv_rho = 1.0 / density

    def keep(index, row):
        coef[index] = jnp.broadcast_to(row, (8, count))

    for d in range(3):
        for a in range(3):
            row = jac_ref[d, a : a + 1, :]
            keep(d * 3 + a, row)
            keep(9 + d * 3 + a, HALF * inv_rho * row)
    keep(18, HALF * lame)
    keep(19, 2.0 * HALF * shear)
    keep(20, HALF * shear)
    azimuth, polar = ang_ref[0], ang_ref[1]
    sin_polar = jnp.sin(polar)
    normal = [jnp.cos(azimuth) * sin_polar, jnp.sin(azimuth) * sin_polar, jnp.cos(polar)]
    weight = (0.5 * FULL) * scale_ref[...]
    for f in range(4):
        for a in range(3):
            keep(21 + f * 3 + a, weight[f : f + 1] * normal[a][f : f + 1])
        keep(37 + f, weight[f : f + 1] * p_speed)
    keep(33, lame)
    keep(34, 2.0 * shear)
    keep(35, shear)
    keep(36, inv_rho)

    ghosts = 256
    locals_all = 4 * count
    row_ids = lax.broadcasted_iota(jnp.int32, (256, count), 0)
    for f in range(4):
        nbr = nbr_ref[f : f + 1, :]
        local = nface_ref[f : f + 1, :] * count + nbr
        outer = jnp.where(nbr < count + ghosts, nbr - count + locals_all, -1)
        index = jnp.where(nbr < count, local, outer)
        for block in range((locals_all + ghosts) // 256):
            hit = (row_ids + block * 256) == index
            onehot[block * 256 : (block + 1) * 256, f * count : (f + 1) * count] = jnp.where(
                hit, 1.0, 0.0
            ).astype(BF16)
    send_ids = lax.broadcasted_iota(jnp.int32, (256, ghosts), 0)
    for block in range(locals_all // 256):
        hit = (send_ids + block * 256) == send_ref[...]
        send_hot[block * 256 : (block + 1) * 256, :] = jnp.where(hit, 1.0, 0.0).astype(BF16)

    q_buf[:, 32:ROWS, :] = jnp.zeros((9, 8, count), F32)
    f_buf[:, 32:ROWS, :] = jnp.zeros((9, 8, count), F32)
    q_buf[:, 0:basis, :] = adj_ref[...]
    b_buf[...] = jnp.zeros_like(b_buf)
    sums[...] = jnp.zeros_like(sums)

    def load_operand(source):
        for field in range(9):
            high, low = split(source[field])
            b_buf[field, 0:ROWS, :] = high
            b_buf[field, KROWS : KROWS + ROWS, :] = low
            b_buf[field, 2 * KROWS : 2 * KROWS + ROWS, :] = high

    def volume(rows):
        for field in range(9):
            y_buf[field, 0:rows, :] = wide_dot(amat_ref[0:rows, :], b_buf[field])

    def advance(factor):
        for t in range(tiles):
            lanes = slice(t * 128, (t + 1) * 128)
            lame_c = coef[18, :, lanes] * factor
            two_c = coef[19, :, lanes] * factor
            shear_c = coef[20, :, lanes] * factor
            for r in range(ROWS // 8):
                rows = slice(r * 8, r * 8 + 8)

                def moved(d, field):
                    return y_buf[field, d * ROWS + r * 8 : d * ROWS + r * 8 + 8, lanes]

                grad = {}
                for b in range(3):
                    parts = [moved(d, 6 + b) for d in range(3)]
                    for a in range(3):
                        grad[a, b] = (
                            coef[a, :, lanes] * parts[0]
                            + coef[3 + a, :, lanes] * parts[1]
                            + coef[6 + a, :, lanes] * parts[2]
                        )
                dil = lame_c * (grad[0, 0] + grad[1, 1] + grad[2, 2])
                for a in range(3):
                    p_buf[a, rows, lanes] = q_buf[a, rows, lanes] - dil - two_c * grad[a, a]
                for field, a, b in ((3, 0, 1), (4, 1, 2), (5, 0, 2)):
                    p_buf[field, rows, lanes] = q_buf[field, rows, lanes] - shear_c * (
                        grad[a, b] + grad[b, a]
                    )
                stress = [[moved(d, field) for d in range(3)] for field in range(6)]
                for b, picks in ((0, (0, 3, 5)), (1, (3, 1, 4)), (2, (5, 4, 2))):
                    total = None
                    for d in range(3):
                        for a in range(3):
                            term = coef[9 + d * 3 + a, :, lanes] * stress[picks[a]][d]
                            total = term if total is None else total + term
                    p_buf[6 + b, rows, lanes] = q_buf[6 + b, rows, lanes] - factor * total

    def element_sums(step):
        for field in range(9):
            f_buf[field, 0:basis, :] = fwd_ref[step, field].astype(F32)
        for t in range(tiles):
            lanes = slice(t * 128, (t + 1) * 128)
            first, second, third = None, None, None
            for r in range(ROWS // 8):
                rows = slice(r * 8, r * 8 + 8)
                x = [p_buf[field, rows, lanes] for field in range(9)]
                y = [f_buf[field, rows, lanes] for field in range(9)]
                one = (x[0] + x[1] + x[2]) * (y[0] + y[1] + y[2])
                two = (x[0] * y[0] + x[1] * y[1] + x[2] * y[2]) + 2.0 * (
                    x[3] * y[3] + x[4] * y[4] + x[5] * y[5]
                )
                three = x[6] * y[6] + x[7] * y[7] + x[8] * y[8]
                first = one if first is None else first + one
                second = two if second is None else second + two
                third = three if third is None else third + three
            sums[0, :, lanes] += first
            sums[1, :, lanes] += second
            sums[2, :, lanes] += third

    def ghost_copy(step, link):
        slot, tile, to_ok, target, from_ok, source = link
        return pltpu.make_async_remote_copy(
            src_ref=send_buf.at[step, tile],
            dst_ref=recv_buf.at[step, slot],
            send_sem=g_send.at[step, slot],
            recv_sem=g_recv.at[step, slot],
            device_id=target,
            device_id_type=MESH,
        )

    pl.semaphore_wait(
        barrier,
        sum(link[2].astype(jnp.int32) for link in links) + target_count(me, n_dev, per_dev),
    )

    def step_body(step, carry):
        load_operand(q_buf)

        def sweep(_, inner):
            volume(3 * ROWS)
            advance(1.0)
            load_operand(p_buf)
            return inner

        lax.fori_loop(0, PICARD, sweep, 0)
        element_sums(step)
        volume(3 * ROWS + 64)
        base = 3 * ROWS
        for field in range(9):
            for g in range(4):
                high, low = split(y_buf[field, base + g * 16 : base + g * 16 + 16, :])
                columns = slice(g * count, (g + 1) * count)
                left_buf[field * 16 : field * 16 + 16, columns] = high
                left_buf[TRACE + field * 16 : TRACE + field * 16 + 16, columns] = low
        picked = wide_dot(left_buf[...], send_hot[...])
        picked = picked[0:TRACE] + picked[TRACE:]
        for tile in range(2):
            send_buf[step, tile] = picked[:, tile * 128 : (tile + 1) * 128]
        for link in links:

            @pl.when(link[2])
            def _(link=link):
                ghost_copy(step, link).start()

        advance(2.0)
        for f in range(4):
            columns = slice(f * count, (f + 1) * count)
            got = wide_dot(left_buf[...], onehot[0:locals_all, columns])
            far_buf[:, columns] = got[0:TRACE] + got[TRACE:]

        for link in links:

            @pl.when(link[4])
            def _(link=link):
                ghost_copy(step, link).wait_recv()

        lane = lax.broadcasted_iota(jnp.int32, (TRACE, 128), 1)
        for tile in range(2):
            both = jnp.where(lane < 64, recv_buf[step, 2 * tile], recv_buf[step, 2 * tile + 1])
            high, low = split(both)
            ghost_left[0:TRACE, tile * 128 : (tile + 1) * 128] = high
            ghost_left[TRACE:, tile * 128 : (tile + 1) * 128] = low
        for f in range(4):
            columns = slice(f * count, (f + 1) * count)
            got = wide_dot(ghost_left[...], onehot[locals_all:, columns])
            far_buf[:, columns] += got[0:TRACE] + got[TRACE:]

        for f in range(4):
            for t in range(tiles):
                lanes = slice(t * 128, (t + 1) * 128)
                far_lanes = slice(f * count + t * 128, f * count + (t + 1) * 128)
                nx, ny, nz = (coef[21 + f * 3 + a, :, lanes] for a in range(3))
                lame_c, two_c = coef[33, :, lanes], coef[34, :, lanes]
                shear_c, inv_c = coef[35, :, lanes], coef[36, :, lanes]
                speed = coef[37 + f, :, lanes]
                for r in range(2):
                    own = [
                        y_buf[k, base + f * 16 + r * 8 : base + f * 16 + r * 8 + 8, lanes]
                        for k in range(9)
                    ]
                    far = [
                        far_buf[k * 16 + r * 8 : k * 16 + r * 8 + 8, far_lanes] for k in range(9)
                    ]
                    x = [own[k] + far[k] for k in range(9)]
                    jump = [speed * (own[k] - far[k]) for k in range(9)]
                    gx, gy, gz = nx * x[6], ny * x[7], nz * x[8]
                    dil = lame_c * (gx + gy + gz)
                    flux = [
                        jump[0] - dil - two_c * gx,
                        jump[1] - dil - two_c * gy,
                        jump[2] - dil - two_c * gz,
                        jump[3] - shear_c * (ny * x[6] + nx * x[7]),
                        jump[4] - shear_c * (nz * x[7] + ny * x[8]),
                        jump[5] - shear_c * (nz * x[6] + nx * x[8]),
                        jump[6] - inv_c * (nx * x[0] + ny * x[3] + nz * x[5]),
                        jump[7] - inv_c * (nx * x[3] + ny * x[1] + nz * x[4]),
                        jump[8] - inv_c * (nx * x[5] + ny * x[4] + nz * x[2]),
                    ]
                    for k in range(9):
                        flux_buf[k, f * 16 + r * 8 : f * 16 + r * 8 + 8, lanes] = flux[k]
        for field in range(9):
            high, low = split(flux_buf[field])
            fx_buf[0:64, :] = high
            fx_buf[64:128, :] = low
            fx_buf[128:192, :] = high
            q_buf[field] = p_buf[field] - wide_dot(lmat_ref[...], fx_buf[...])
        for link in links:

            @pl.when(link[2])
            def _(link=link):
                ghost_copy(step, link).wait_send()

        return carry

    lax.fori_loop(0, steps, step_body, 0)
    out_ref[...] = q_buf[:, 0:basis, :]

    parts = [jnp.sum(sums[k], axis=0, keepdims=True) for k in range(3)]
    first, second, third = parts
    gain = KERNEL_WEIGHT * FULL
    square = s_speed * s_speed
    terms = [
        gain * (2.0 * density * p_speed * first),
        gain * (density * s_speed * (2.0 * second - 4.0 * first)),
        gain * ((p_speed * p_speed - 2.0 * square) * first + square * second + third),
    ]
    term_row = lax.broadcasted_iota(jnp.int32, (8, count), 0)
    stacked = jnp.where(term_row == 0, terms[0], 0.0)
    stacked = jnp.where(term_row == 1, terms[1], stacked)
    stacked = jnp.where(term_row == 2, terms[2], stacked)
    entry = cell_ref[...]
    owner = lax.shift_right_logical(entry, per_dev.bit_length() - 1)
    coarse = (entry - owner * per_dev) * n_dev + owner
    relative = coarse - (per_dev * me - 1)
    hot = jnp.where(
        lax.broadcasted_iota(jnp.int32, (128, count), 0) == relative, 1.0, 0.0
    ).astype(F32)
    cells_out[...] = lax.dot_general(
        stacked,
        hot,
        (((1,), (1,)), ((), ())),
        precision=lax.Precision.HIGHEST,
        preferred_element_type=F32,
    )

    def cell_copy(c, cell, dst, sem):
        target = lax.rem(cell, n_dev)
        slot = lax.div(cell, n_dev)
        return pltpu.make_async_remote_copy(
            src_ref=cells_out,
            dst_ref=dst.at[slot],
            send_sem=h_send.at[c],
            recv_sem=sem.at[slot],
            device_id=place(target),
            device_id_type=MESH,
        )

    def to_cell(c, cell, dst, sem):
        target = lax.rem(cell, n_dev)
        slot = lax.div(cell, n_dev)

        @pl.when(target != me)
        def _():
            cell_copy(c, cell, dst, sem).start()

        @pl.when(target == me)
        def _():
            dst[slot] = cells_out[...]

    low_cell = per_dev * me - 1
    high_cell = per_dev * me + per_dev

    def send_main(c, carry):
        to_cell(c, per_dev * me + c, cells_main, h_recv_main)
        return carry

    lax.fori_loop(0, per_dev, send_main, 0)

    @pl.when(me > 0)
    def _():
        to_cell(per_dev, low_cell, cells_side, h_recv_side)

    @pl.when(me < n_dev - 1)
    def _():
        to_cell(per_dev + 1, high_cell, cells_side, h_recv_side)

    def finish(j, carry):
        @pl.when(main_source(j) != me)
        def _():
            pltpu.make_async_copy(cells_out, cells_main.at[j], h_recv_main.at[j]).wait()

        exists, side = side_source(j)

        @pl.when(jnp.logical_and(exists, side != me))
        def _():
            pltpu.make_async_copy(cells_out, cells_side.at[j], h_recv_side.at[j]).wait()

        return carry

    lax.fori_loop(0, per_dev, finish, 0)

    lane = lax.broadcasted_iota(jnp.int32, (8, 128), 1)
    inner = lax.rem(me, per_dev)
    main_lane = inner + 1
    side_lane = jnp.where(inner == 0, per_dev + 1, 0)
    result = jnp.zeros((8, 128), F32)
    for j in range(per_dev):
        value = jnp.where(lane == main_lane, cells_main[j], 0.0)
        value = value + jnp.where(lane == side_lane, cells_side[j], 0.0)
        result = jnp.where(lane == j, jnp.sum(value, axis=1, keepdims=True), result)
    hist_ref[...] = result[0:3, 0:per_dev]

    def drain(c, carry):
        @pl.when(lax.rem(per_dev * me + c, n_dev) != me)
        def _():
            pltpu.make_async_copy(cells_out, cells_main.at[0], h_send.at[c]).wait()

        return carry

    lax.fori_loop(0, per_dev, drain, 0)

    @pl.when(jnp.logical_and(me > 0, lax.rem(jnp.maximum(low_cell, 0), n_dev) != me))
    def _():
        pltpu.make_async_copy(cells_out, cells_side.at[0], h_send.at[per_dev]).wait()

    @pl.when(jnp.logical_and(me < n_dev - 1, lax.rem(high_cell, n_dev) != me))
    def _():
        pltpu.make_async_copy(cells_out, cells_side.at[0], h_send.at[per_dev + 1]).wait()


def target_count(me, n_dev, per_dev):
    total = jnp.int32(0)
    for c in range(per_dev):
        total = total + (lax.rem(per_dev * me + c, n_dev) != me).astype(jnp.int32)
    low_cell = per_dev * me - 1
    high_cell = per_dev * me + per_dev
    low = jnp.logical_and(me > 0, lax.rem(jnp.maximum(low_cell, 0), n_dev) != me)
    high = jnp.logical_and(me < n_dev - 1, lax.rem(high_cell, n_dev) != me)
    return total + low.astype(jnp.int32) + high.astype(jnp.int32)


def three_way(matrix):
    high = lax.reduce_precision(matrix, 8, 7)
    low = matrix - high
    return jnp.concatenate([high, high, low], axis=1).astype(BF16)


def shards(
    n_depth,
    n_map,
    adjoint,
    forward,
    p_speed,
    s_speed,
    density,
    inv_jacobian,
    face_angles,
    face_scale,
    stiffness,
    face_basis,
    neighbours,
    neighbour_face,
    send_elements,
    send_faces,
    cell_index,
):
    basis, fields, count = adjoint.shape
    steps = forward.shape[0]
    modes = face_basis.shape[2]
    per_dev = count // 32
    moving = jnp.pad(
        jnp.transpose(stiffness, (0, 2, 1)), ((0, 0), (0, ROWS - basis), (0, KROWS - basis))
    ).reshape(3 * ROWS, KROWS)
    tracing = jnp.pad(
        jnp.transpose(face_basis, (0, 2, 1)), ((0, 0), (0, 16 - modes), (0, KROWS - basis))
    ).reshape(64, KROWS)
    amat = three_way(jnp.concatenate([moving, tracing], axis=0))
    lifting = jnp.pad(
        jnp.transpose(face_basis, (1, 0, 2)), ((0, ROWS - basis), (0, 0), (0, 16 - modes))
    ).reshape(ROWS, 64)
    lmat = three_way(lifting)
    send_index = (send_faces * count + send_elements).reshape(1, 256)
    row = lambda value: value.reshape(1, count)
    vmem = pl.BlockSpec(memory_space=pltpu.VMEM)
    state, kernels = pl.pallas_call(
        functools.partial(kernel, n_depth, n_map),
        out_shape=(
            jax.ShapeDtypeStruct((fields, basis, count), F32),
            jax.ShapeDtypeStruct((3, per_dev), F32),
        ),
        in_specs=[vmem] * 14,
        out_specs=(vmem, vmem),
        scratch_shapes=[
            pltpu.VMEM((9, ROWS, count), F32),
            pltpu.VMEM((9, ROWS, count), F32),
            pltpu.VMEM((9, 3 * KROWS, count), BF16),
            pltpu.VMEM((9, 3 * ROWS + 64, count), F32),
            pltpu.VMEM((9, ROWS, count), F32),
            pltpu.VMEM((41, 8, count), F32),
            pltpu.VMEM((4 * count + 256, 4 * count), BF16),
            pltpu.VMEM((4 * count, 256), BF16),
            pltpu.VMEM((2 * TRACE, 4 * count), BF16),
            pltpu.VMEM((2 * TRACE, 256), BF16),
            pltpu.VMEM((TRACE, 4 * count), F32),
            pltpu.VMEM((9, 64, count), F32),
            pltpu.VMEM((192, count), BF16),
            pltpu.VMEM((3, 8, count), F32),
            pltpu.VMEM((steps, 2, TRACE, 128), F32),
            pltpu.VMEM((steps, 4, TRACE, 128), F32),
            pltpu.VMEM((8, 128), F32),
            pltpu.VMEM((per_dev, 8, 128), F32),
            pltpu.VMEM((per_dev, 8, 128), F32),
            pltpu.SemaphoreType.DMA((steps, 4)),
            pltpu.SemaphoreType.DMA((steps, 4)),
            pltpu.SemaphoreType.DMA((per_dev + 2,)),
            pltpu.SemaphoreType.DMA((per_dev,)),
            pltpu.SemaphoreType.DMA((per_dev,)),
        ],
        compiler_params=pltpu.CompilerParams(
            collective_id=0, has_side_effects=True, vmem_limit_bytes=56 * 1024 * 1024
        ),
    )(
        jnp.transpose(adjoint, (1, 0, 2)),
        jnp.transpose(forward, (0, 2, 1, 3)),
        row(p_speed),
        row(s_speed),
        row(density),
        inv_jacobian,
        face_angles,
        face_scale,
        amat,
        lmat,
        neighbours,
        neighbour_face,
        send_index,
        row(cell_index),
    )
    return jnp.transpose(state, (1, 0, 2)), kernels


def solution(mesh):
    n_depth, n_map = mesh.shape["depth"], mesh.shape["map"]
    both = ("depth", "map")
    placed = (
        P(None, None, both),
        P(None, None, None, both),
        P(both),
        P(both),
        P(both),
        P(None, None, both),
        P(None, None, both),
        P(None, both),
        P(),
        P(),
        P(None, both),
        P(None, both),
        P(None, both),
        P(None, both),
        P(both),
    )
    return jax.shard_map(
        functools.partial(shards, n_depth, n_map),
        mesh=mesh,
        in_specs=placed,
        out_specs=(P(None, None, both), P(None, both)),
        check_vma=False,
    )
```

```python
import functools

import jax
import jax.numpy as jnp
from jax import lax
from jax.experimental import pallas as pl
from jax.experimental.pallas import tpu as pltpu
from jax.sharding import PartitionSpec as P

MESH = pl.DeviceIdType.MESH
PICARD = 4
HALF = 0.15
FULL = 0.3
KERNEL_WEIGHT = 0.125
F32 = jnp.float32
BF16 = jnp.bfloat16
ROWS = 40
KROWS = 48
TRACE = 144


def split(value):
    high = value.astype(BF16)
    low = (value - high.astype(F32)).astype(BF16)
    return high, low


def wide_dot(left, right):
    return jnp.dot(left, right, preferred_element_type=F32)


def kernel(
    n_depth,
    n_map,
    adj_ref,
    fwd_ref,
    p_ref,
    s_ref,
    rho_ref,
    jac_ref,
    ang_ref,
    scale_ref,
    stiff_ref,
    face_ref,
    nbr_ref,
    nface_ref,
    send_ref,
    sface_ref,
    cell_ref,
    out_ref,
    hist_ref,
    amat_ref,
    lmat_ref,
    square,
    send_row,
    q_buf,
    p_buf,
    b_buf,
    y_buf,
    f_buf,
    coef,
    onehot,
    send_hot,
    left_buf,
    ghost_left,
    far_buf,
    flux_buf,
    fx_buf,
    sums,
    send_buf,
    recv_buf,
    cells_out,
    cells_main,
    cells_side,
    g_send,
    g_recv,
    h_send,
    h_recv_main,
    h_recv_side,
):
    n_dev = n_depth * n_map
    count = adj_ref.shape[2]
    basis = adj_ref.shape[1]
    steps = fwd_ref.shape[0]
    tiles = count // 128
    per_dev = count // 32
    total_cells = per_dev * n_dev
    own_i = lax.axis_index("depth")
    own_j = lax.axis_index("map")
    me = own_i * n_map + own_j

    def place(linear):
        return (lax.div(linear, n_map), lax.rem(linear, n_map))

    links = [
        (0, 0, own_i < n_depth - 1, (own_i + 1, own_j), own_i > 0, (own_i - 1, own_j)),
        (1, 0, own_i > 0, (own_i - 1, own_j), own_i < n_depth - 1, (own_i + 1, own_j)),
        (2, 1, own_j < n_map - 1, (own_i, own_j + 1), own_j > 0, (own_i, own_j - 1)),
        (3, 1, own_j > 0, (own_i, own_j - 1), own_j < n_map - 1, (own_i, own_j + 1)),
    ]

    recv_buf[...] = jnp.zeros_like(recv_buf)
    cells_main[...] = jnp.zeros_like(cells_main)
    cells_side[...] = jnp.zeros_like(cells_side)

    barrier = pltpu.get_barrier_semaphore()
    for slot, tile, to_ok, target, from_ok, source in links:

        @pl.when(from_ok)
        def _(source=source):
            pl.semaphore_signal(barrier, inc=1, device_id=source, device_id_type=MESH)

    def main_source(j):
        return lax.div(me + n_dev * j, per_dev)

    def side_source(j):
        cell = me + n_dev * j
        place_in = lax.rem(cell, per_dev)
        home = lax.div(cell, per_dev)
        below = jnp.logical_and(place_in == 0, home > 0)
        above = jnp.logical_and(place_in == per_dev - 1, home < n_dev - 1)
        source = jnp.where(below, home - 1, home + 1)
        return jnp.logical_or(below, above), jnp.clip(source, 0, n_dev - 1)

    def greet(j, carry):
        main = main_source(j)

        @pl.when(main != me)
        def _():
            pl.semaphore_signal(barrier, inc=1, device_id=place(main), device_id_type=MESH)

        exists, side = side_source(j)

        @pl.when(jnp.logical_and(exists, side != me))
        def _():
            pl.semaphore_signal(barrier, inc=1, device_id=place(side), device_id_type=MESH)

        return carry

    lax.fori_loop(0, per_dev, greet, 0)

    three_zero = jnp.zeros((128, 256), F32)

    def three_parts(matrix, step_lanes, rows):
        square[0, 0:rows, 0:128] = matrix[0:rows]
        high, low = split(square[0, 0:rows, :])
        high, low = high.astype(F32), low.astype(F32)
        joined = high + pltpu.roll(high, step_lanes, 1) + pltpu.roll(low, 2 * step_lanes, 1)
        return joined.astype(BF16)

    square[0] = three_zero
    for d in range(3):
        square[1] = three_zero
        square[1, 0:basis, 0:basis] = stiff_ref[d]
        flipped = square[1, :, 0:128].T
        amat_ref[d * ROWS : (d + 1) * ROWS, :] = three_parts(flipped, KROWS, ROWS)
    square[1] = three_zero
    for g in range(4):
        square[1, g * 16 : g * 16 + face_ref.shape[0], 0:basis] = face_ref[:, g, :]
    tracing = square[1, :, 0:128]
    amat_ref[3 * ROWS : 3 * ROWS + 64, :] = three_parts(tracing, KROWS, 64)
    lmat_ref[...] = three_parts(tracing.T, 64, ROWS)

    p_speed, s_speed, density = p_ref[...], s_ref[...], rho_ref[...]
    lame = density * (p_speed * p_speed - 2.0 * s_speed * s_speed)
    shear = density * s_speed * s_speed
    inv_rho = 1.0 / density

    def keep(index, row):
        coef[index] = jnp.broadcast_to(row, (8, count))

    for d in range(3):
        for a in range(3):
            row = jac_ref[d, a : a + 1, :]
            keep(d * 3 + a, row)
            keep(9 + d * 3 + a, HALF * inv_rho * row)
    keep(18, HALF * lame)
    keep(19, 2.0 * HALF * shear)
    keep(20, HALF * shear)
    azimuth, polar = ang_ref[0], ang_ref[1]
    sin_polar = jnp.sin(polar)
    normal = [jnp.cos(azimuth) * sin_polar, jnp.sin(azimuth) * sin_polar, jnp.cos(polar)]
    weight = (0.5 * FULL) * scale_ref[...]
    for f in range(4):
        for a in range(3):
            keep(21 + f * 3 + a, weight[f : f + 1] * normal[a][f : f + 1])
        keep(37 + f, weight[f : f + 1] * p_speed)
    keep(33, lame)
    keep(34, 2.0 * shear)
    keep(35, shear)
    keep(36, inv_rho)

    ghosts = 256
    locals_all = 4 * count
    row_ids = lax.broadcasted_iota(jnp.int32, (256, count), 0)
    for f in range(4):
        nbr = nbr_ref[f : f + 1, :]
        local = nface_ref[f : f + 1, :] * count + nbr
        outer = jnp.where(nbr < count + ghosts, nbr - count + locals_all, -1)
        index = jnp.where(nbr < count, local, outer)
        for block in range((locals_all + ghosts) // 256):
            hit = (row_ids + block * 256) == index
            onehot[block * 256 : (block + 1) * 256, f * count : (f + 1) * count] = jnp.where(
                hit, 1.0, 0.0
            ).astype(BF16)
    send_row[...] = jnp.zeros_like(send_row)
    send_row[0:4, 0:64] = sface_ref[...] * count + send_ref[...]
    send_lane = lax.broadcasted_iota(jnp.int32, (8, 128), 1)
    shifted = pltpu.roll(send_row[...], 64, 1)
    send_ids = lax.broadcasted_iota(jnp.int32, (256, 128), 0)
    for tile in range(2):
        index = jnp.where(
            send_lane[0:1] < 64, send_row[2 * tile : 2 * tile + 1, :], shifted[2 * tile + 1 : 2 * tile + 2]
        )
        for block in range(locals_all // 256):
            hit = (send_ids + block * 256) == index
            send_hot[block * 256 : (block + 1) * 256, tile * 128 : (tile + 1) * 128] = jnp.where(
                hit, 1.0, 0.0
            ).astype(BF16)

    q_buf[:, 32:ROWS, :] = jnp.zeros((9, 8, count), F32)
    f_buf[:, 32:ROWS, :] = jnp.zeros((9, 8, count), F32)
    q_buf[:, 0:basis, :] = adj_ref[...]
    b_buf[...] = jnp.zeros_like(b_buf)
    sums[...] = jnp.zeros_like(sums)

    half = count // 2
    halves = (slice(0, half), slice(half, count))

    def load_operand(source, h):
        for field in range(9):
            high, low = split(source[field, :, halves[h]])
            b_buf[field, 0:ROWS, halves[h]] = high
            b_buf[field, KROWS : KROWS + ROWS, halves[h]] = low
            b_buf[field, 2 * KROWS : 2 * KROWS + ROWS, halves[h]] = high

    def volume(field, h, start=0, stop=3 * ROWS):
        y_buf[field, start:stop, halves[h]] = wide_dot(
            amat_ref[start:stop, 0 : 3 * KROWS], b_buf[field, :, halves[h]]
        )

    def advance(factor, h):
        for t in range(h * tiles // 2, (h + 1) * tiles // 2):
            lanes = slice(t * 128, (t + 1) * 128)
            lame_c = coef[18, :, lanes] * factor
            two_c = coef[19, :, lanes] * factor
            shear_c = coef[20, :, lanes] * factor
            for r in range(ROWS // 8):
                rows = slice(r * 8, r * 8 + 8)

                def moved(d, field):
                    return y_buf[field, d * ROWS + r * 8 : d * ROWS + r * 8 + 8, lanes]

                grad = {}
                for b in range(3):
                    parts = [moved(d, 6 + b) for d in range(3)]
                    for a in range(3):
                        grad[a, b] = (
                            coef[a, :, lanes] * parts[0]
                            + coef[3 + a, :, lanes] * parts[1]
                            + coef[6 + a, :, lanes] * parts[2]
                        )
                dil = lame_c * (grad[0, 0] + grad[1, 1] + grad[2, 2])
                for a in range(3):
                    p_buf[a, rows, lanes] = q_buf[a, rows, lanes] - dil - two_c * grad[a, a]
                for field, a, b in ((3, 0, 1), (4, 1, 2), (5, 0, 2)):
                    p_buf[field, rows, lanes] = q_buf[field, rows, lanes] - shear_c * (
                        grad[a, b] + grad[b, a]
                    )
                stress = [[moved(d, field) for d in range(3)] for field in range(6)]
                for b, picks in ((0, (0, 3, 5)), (1, (3, 1, 4)), (2, (5, 4, 2))):
                    total = None
                    for d in range(3):
                        for a in range(3):
                            term = coef[9 + d * 3 + a, :, lanes] * stress[picks[a]][d]
                            total = term if total is None else total + term
                    p_buf[6 + b, rows, lanes] = q_buf[6 + b, rows, lanes] - factor * total
                yield

    def element_sums(step):
        for field in range(9):
            f_buf[field, 0:basis, :] = fwd_ref[step, field].astype(F32)
        for t in range(tiles):
            lanes = slice(t * 128, (t + 1) * 128)
            first, second, third = None, None, None
            for r in range(ROWS // 8):
                rows = slice(r * 8, r * 8 + 8)
                x = [p_buf[field, rows, lanes] for field in range(9)]
                y = [f_buf[field, rows, lanes] for field in range(9)]
                one = (x[0] + x[1] + x[2]) * (y[0] + y[1] + y[2])
                two = (x[0] * y[0] + x[1] * y[1] + x[2] * y[2]) + 2.0 * (
                    x[3] * y[3] + x[4] * y[4] + x[5] * y[5]
                )
                three = x[6] * y[6] + x[7] * y[7] + x[8] * y[8]
                first = one if first is None else first + one
                second = two if second is None else second + two
                third = three if third is None else third + three
            sums[0, :, lanes] += first
            sums[1, :, lanes] += second
            sums[2, :, lanes] += third
            yield

    def ghost_copy(step, link):
        slot, tile, to_ok, target, from_ok, source = link
        return pltpu.make_async_remote_copy(
            src_ref=send_buf.at[step, tile],
            dst_ref=recv_buf.at[step, slot],
            send_sem=g_send.at[step, slot],
            recv_sem=g_recv.at[step, slot],
            device_id=target,
            device_id_type=MESH,
        )

    pl.semaphore_wait(
        barrier,
        sum(link[2].astype(jnp.int32) for link in links) + target_count(me, n_dev, per_dev),
    )

    def cell_copy(c, cell, dst, sem):
        target = lax.rem(cell, n_dev)
        slot = lax.div(cell, n_dev)
        return pltpu.make_async_remote_copy(
            src_ref=cells_out,
            dst_ref=dst.at[slot],
            send_sem=h_send.at[c],
            recv_sem=sem.at[slot],
            device_id=place(target),
            device_id_type=MESH,
        )

    def to_cell(c, cell, dst, sem):
        target = lax.rem(cell, n_dev)
        slot = lax.div(cell, n_dev)

        @pl.when(target != me)
        def _():
            cell_copy(c, cell, dst, sem).start()

        @pl.when(target == me)
        def _():
            dst[slot] = cells_out[...]

    low_cell = per_dev * me - 1
    high_cell = per_dev * me + per_dev

    def send_cells():
        parts = [jnp.sum(sums[k], axis=0, keepdims=True) for k in range(3)]
        first, second, third = parts
        gain = KERNEL_WEIGHT * FULL
        speed_sq = s_speed * s_speed
        terms = [
            gain * (2.0 * density * p_speed * first),
            gain * (density * s_speed * (2.0 * second - 4.0 * first)),
            gain * ((p_speed * p_speed - 2.0 * speed_sq) * first + speed_sq * second + third),
        ]
        term_row = lax.broadcasted_iota(jnp.int32, (8, count), 0)
        stacked = jnp.where(term_row == 0, terms[0], 0.0)
        stacked = jnp.where(term_row == 1, terms[1], stacked)
        stacked = jnp.where(term_row == 2, terms[2], stacked)
        entry = cell_ref[...]
        owner = lax.shift_right_logical(entry, per_dev.bit_length() - 1)
        coarse = (entry - owner * per_dev) * n_dev + owner
        relative = coarse - (per_dev * me - 1)
        hot = jnp.where(
            lax.broadcasted_iota(jnp.int32, (128, count), 0) == relative, 1.0, 0.0
        ).astype(F32)
        cells_out[...] = lax.dot_general(
            stacked,
            hot,
            (((1,), (1,)), ((), ())),
            precision=lax.Precision.HIGHEST,
            preferred_element_type=F32,
        )

        def send_main(c, carry):
            to_cell(c, per_dev * me + c, cells_main, h_recv_main)
            return carry

        lax.fori_loop(0, per_dev, send_main, 0)

        @pl.when(me > 0)
        def _():
            to_cell(per_dev, low_cell, cells_side, h_recv_side)

        @pl.when(me < n_dev - 1)
        def _():
            to_cell(per_dev + 1, high_cell, cells_side, h_recv_side)

    def step_body(step, carry):
        load_operand(q_buf, 0)
        load_operand(q_buf, 1)
        base = 3 * ROWS
        for field in range(9):
            volume(field, 0)

        def sweep(_, inner):
            for h in range(2):
                pieces = advance(1.0, h)
                for field in range(9):
                    volume(field, 1 - h)
                    next(pieces)
                for _ in pieces:
                    pass
                load_operand(p_buf, h)
            return inner

        lax.fori_loop(0, PICARD, sweep, 0)
        for field in range(9):
            volume(field, 0, base, base + 64)
            volume(field, 1, 0, base + 64)
        for _ in element_sums(step):
            pass
        for field in range(9):
            for g in range(4):
                high, low = split(y_buf[field, base + g * 16 : base + g * 16 + 16, :])
                columns = slice(g * count, (g + 1) * count)
                left_buf[field * 16 : field * 16 + 16, columns] = high
                left_buf[TRACE + field * 16 : TRACE + field * 16 + 16, columns] = low
        picked = wide_dot(left_buf[...], send_hot[...])
        picked = picked[0:TRACE] + picked[TRACE:]
        for tile in range(2):
            send_buf[step, tile] = picked[:, tile * 128 : (tile + 1) * 128]
        for link in links:

            @pl.when(link[2])
            def _(link=link):
                ghost_copy(step, link).start()

        @pl.when(step == steps - 1)
        def _():
            send_cells()

        def side_work():
            yield from advance(2.0, 0)
            yield from advance(2.0, 1)

        work = side_work()
        for c in range(8):
            columns = slice(c * half, (c + 1) * half)
            got = wide_dot(left_buf[...], onehot[0:locals_all, columns])
            far_buf[:, columns] = got[0:TRACE] + got[TRACE:]
            for _ in range(3):
                next(work, None)
        for _ in work:
            pass

        for link in links:

            @pl.when(link[4])
            def _(link=link):
                ghost_copy(step, link).wait_recv()

        lane = lax.broadcasted_iota(jnp.int32, (TRACE, 128), 1)
        for tile in range(2):
            both = jnp.where(lane < 64, recv_buf[step, 2 * tile], recv_buf[step, 2 * tile + 1])
            high, low = split(both)
            ghost_left[0:TRACE, tile * 128 : (tile + 1) * 128] = high
            ghost_left[TRACE:, tile * 128 : (tile + 1) * 128] = low
        for f in range(4):
            columns = slice(f * count, (f + 1) * count)
            got = wide_dot(ghost_left[...], onehot[locals_all:, columns])
            far_buf[:, columns] += got[0:TRACE] + got[TRACE:]

        for f in range(4):
            for t in range(tiles):
                lanes = slice(t * 128, (t + 1) * 128)
                far_lanes = slice(f * count + t * 128, f * count + (t + 1) * 128)
                nx, ny, nz = (coef[21 + f * 3 + a, :, lanes] for a in range(3))
                lame_c, two_c = coef[33, :, lanes], coef[34, :, lanes]
                shear_c, inv_c = coef[35, :, lanes], coef[36, :, lanes]
                speed = coef[37 + f, :, lanes]
                for r in range(2):
                    own = [
                        y_buf[k, base + f * 16 + r * 8 : base + f * 16 + r * 8 + 8, lanes]
                        for k in range(9)
                    ]
                    far = [
                        far_buf[k * 16 + r * 8 : k * 16 + r * 8 + 8, far_lanes] for k in range(9)
                    ]
                    x = [own[k] + far[k] for k in range(9)]
                    jump = [speed * (own[k] - far[k]) for k in range(9)]
                    gx, gy, gz = nx * x[6], ny * x[7], nz * x[8]
                    dil = lame_c * (gx + gy + gz)
                    flux = [
                        jump[0] - dil - two_c * gx,
                        jump[1] - dil - two_c * gy,
                        jump[2] - dil - two_c * gz,
                        jump[3] - shear_c * (ny * x[6] + nx * x[7]),
                        jump[4] - shear_c * (nz * x[7] + ny * x[8]),
                        jump[5] - shear_c * (nz * x[6] + nx * x[8]),
                        jump[6] - inv_c * (nx * x[0] + ny * x[3] + nz * x[5]),
                        jump[7] - inv_c * (nx * x[3] + ny * x[1] + nz * x[4]),
                        jump[8] - inv_c * (nx * x[5] + ny * x[4] + nz * x[2]),
                    ]
                    for k in range(9):
                        flux_buf[k, f * 16 + r * 8 : f * 16 + r * 8 + 8, lanes] = flux[k]
        for field in range(9):
            high, low = split(flux_buf[field])
            fx_buf[0:64, :] = high
            fx_buf[64:128, :] = low
            fx_buf[128:192, :] = high
            q_buf[field] = p_buf[field] - wide_dot(lmat_ref[:, 0:192], fx_buf[...])
        for link in links:

            @pl.when(link[2])
            def _(link=link):
                ghost_copy(step, link).wait_send()

        return carry

    lax.fori_loop(0, steps, step_body, 0)
    out_ref[...] = q_buf[:, 0:basis, :]

    def finish(j, carry):
        @pl.when(main_source(j) != me)
        def _():
            pltpu.make_async_copy(cells_out, cells_main.at[j], h_recv_main.at[j]).wait()

        exists, side = side_source(j)

        @pl.when(jnp.logical_and(exists, side != me))
        def _():
            pltpu.make_async_copy(cells_out, cells_side.at[j], h_recv_side.at[j]).wait()

        return carry

    lax.fori_loop(0, per_dev, finish, 0)

    lane = lax.broadcasted_iota(jnp.int32, (8, 128), 1)
    inner = lax.rem(me, per_dev)
    main_lane = inner + 1
    side_lane = jnp.where(inner == 0, per_dev + 1, 0)
    result = jnp.zeros((8, 128), F32)
    for j in range(per_dev):
        value = jnp.where(lane == main_lane, cells_main[j], 0.0)
        value = value + jnp.where(lane == side_lane, cells_side[j], 0.0)
        result = jnp.where(lane == j, jnp.sum(value, axis=1, keepdims=True), result)
    hist_ref[...] = result[0:3, 0:per_dev]

    def drain(c, carry):
        @pl.when(lax.rem(per_dev * me + c, n_dev) != me)
        def _():
            pltpu.make_async_copy(cells_out, cells_main.at[0], h_send.at[c]).wait()

        return carry

    lax.fori_loop(0, per_dev, drain, 0)

    @pl.when(jnp.logical_and(me > 0, lax.rem(jnp.maximum(low_cell, 0), n_dev) != me))
    def _():
        pltpu.make_async_copy(cells_out, cells_side.at[0], h_send.at[per_dev]).wait()

    @pl.when(jnp.logical_and(me < n_dev - 1, lax.rem(high_cell, n_dev) != me))
    def _():
        pltpu.make_async_copy(cells_out, cells_side.at[0], h_send.at[per_dev + 1]).wait()


def target_count(me, n_dev, per_dev):
    total = jnp.int32(0)
    for c in range(per_dev):
        total = total + (lax.rem(per_dev * me + c, n_dev) != me).astype(jnp.int32)
    low_cell = per_dev * me - 1
    high_cell = per_dev * me + per_dev
    low = jnp.logical_and(me > 0, lax.rem(jnp.maximum(low_cell, 0), n_dev) != me)
    high = jnp.logical_and(me < n_dev - 1, lax.rem(high_cell, n_dev) != me)
    return total + low.astype(jnp.int32) + high.astype(jnp.int32)


def hand_over(state_ref, cells_ref, out_ref, hist_ref):
    out_ref[...] = state_ref[...]
    hist_ref[...] = cells_ref[...]


def shards(
    n_depth,
    n_map,
    adjoint,
    forward,
    p_speed,
    s_speed,
    density,
    inv_jacobian,
    face_angles,
    face_scale,
    stiffness,
    face_basis,
    neighbours,
    neighbour_face,
    send_elements,
    send_faces,
    cell_index,
):
    basis, fields, count = adjoint.shape
    steps = forward.shape[0]
    per_dev = count // 32
    row = lambda value: value.reshape(1, count)
    vmem = pl.BlockSpec(memory_space=pltpu.VMEM)
    state, kernels = pl.pallas_call(
        functools.partial(kernel, n_depth, n_map),
        out_shape=(
            jax.ShapeDtypeStruct((fields, basis, count), F32),
            jax.ShapeDtypeStruct((3, per_dev), F32),
        ),
        in_specs=[vmem] * 15,
        out_specs=(vmem, vmem),
        scratch_shapes=[
            pltpu.VMEM((3 * ROWS + 64, 256), BF16),
            pltpu.VMEM((ROWS, 256), BF16),
            pltpu.VMEM((2, 128, 256), F32),
            pltpu.VMEM((8, 128), jnp.int32),
            pltpu.VMEM((9, ROWS, count), F32),
            pltpu.VMEM((9, ROWS, count), F32),
            pltpu.VMEM((9, 3 * KROWS, count), BF16),
            pltpu.VMEM((9, 3 * ROWS + 64, count), F32),
            pltpu.VMEM((9, ROWS, count), F32),
            pltpu.VMEM((41, 8, count), F32),
            pltpu.VMEM((4 * count + 256, 4 * count), BF16),
            pltpu.VMEM((4 * count, 256), BF16),
            pltpu.VMEM((2 * TRACE, 4 * count), BF16),
            pltpu.VMEM((2 * TRACE, 256), BF16),
            pltpu.VMEM((TRACE, 4 * count), F32),
            pltpu.VMEM((9, 64, count), F32),
            pltpu.VMEM((192, count), BF16),
            pltpu.VMEM((3, 8, count), F32),
            pltpu.VMEM((steps, 2, TRACE, 128), F32),
            pltpu.VMEM((steps, 4, TRACE, 128), F32),
            pltpu.VMEM((8, 128), F32),
            pltpu.VMEM((per_dev, 8, 128), F32),
            pltpu.VMEM((per_dev, 8, 128), F32),
            pltpu.SemaphoreType.DMA((steps, 4)),
            pltpu.SemaphoreType.DMA((steps, 4)),
            pltpu.SemaphoreType.DMA((per_dev + 2,)),
            pltpu.SemaphoreType.DMA((per_dev,)),
            pltpu.SemaphoreType.DMA((per_dev,)),
        ],
        compiler_params=pltpu.CompilerParams(
            collective_id=0, has_side_effects=True, vmem_limit_bytes=36 * 1024 * 1024
        ),
    )(
        jnp.transpose(adjoint, (1, 0, 2)),
        jnp.transpose(forward, (0, 2, 1, 3)),
        row(p_speed),
        row(s_speed),
        row(density),
        inv_jacobian,
        face_angles,
        face_scale,
        stiffness,
        jnp.transpose(face_basis, (2, 0, 1)),
        neighbours,
        neighbour_face,
        send_elements,
        send_faces,
        row(cell_index),
    )
    state, kernels = pl.pallas_call(
        hand_over,
        out_shape=(
            jax.ShapeDtypeStruct(state.shape, F32),
            jax.ShapeDtypeStruct(kernels.shape, F32),
        ),
        in_specs=[vmem] * 2,
        out_specs=(vmem, vmem),
    )(state, kernels)
    return jnp.transpose(state, (1, 0, 2)), kernels


def solution(mesh):
    n_depth, n_map = mesh.shape["depth"], mesh.shape["map"]
    both = ("depth", "map")
    placed = (
        P(None, None, both),
        P(None, None, None, both),
        P(both),
        P(both),
        P(both),
        P(None, None, both),
        P(None, None, both),
        P(None, both),
        P(),
        P(),
        P(None, both),
        P(None, both),
        P(None, both),
        P(None, both),
        P(both),
    )
    return jax.shard_map(
        functools.partial(shards, n_depth, n_map),
        mesh=mesh,
        in_specs=placed,
        out_specs=(P(None, None, both), P(None, both)),
        check_vma=False,
    )
```

```python
import functools

import jax
import jax.numpy as jnp
from jax import lax
from jax.experimental import pallas as pl
from jax.experimental.pallas import tpu as pltpu
from jax.sharding import PartitionSpec as P

MESH = pl.DeviceIdType.MESH
PICARD = 4
HALF = 0.15
FULL = 0.3
KERNEL_WEIGHT = 0.125
F32 = jnp.float32
BF16 = jnp.bfloat16
ROWS = 40
KROWS = 48
TRACE = 144


def split(value):
    high = value.astype(BF16)
    low = (value - high.astype(F32)).astype(BF16)
    return high, low


def wide_dot(left, right):
    return jnp.dot(left, right, preferred_element_type=F32)


def kernel(
    n_depth,
    n_map,
    adj_ref,
    fwd_ref,
    p_ref,
    s_ref,
    rho_ref,
    jac_ref,
    ang_ref,
    scale_ref,
    stiff_ref,
    face_ref,
    nbr_ref,
    nface_ref,
    send_ref,
    sface_ref,
    cell_ref,
    out_ref,
    hist_ref,
    amat_ref,
    lmat_ref,
    square,
    send_row,
    q_buf,
    p_buf,
    b_buf,
    y_buf,
    f_buf,
    coef,
    onehot,
    send_hot,
    left_buf,
    ghost_left,
    far_buf,
    flux_buf,
    fx_buf,
    sums,
    send_buf,
    recv_buf,
    cells_out,
    cells_main,
    cells_side,
    g_send,
    g_recv,
    h_send,
    h_recv_main,
    h_recv_side,
):
    n_dev = n_depth * n_map
    count = adj_ref.shape[2]
    basis = adj_ref.shape[1]
    steps = fwd_ref.shape[0]
    tiles = count // 128
    per_dev = count // 32
    total_cells = per_dev * n_dev
    own_i = lax.axis_index("depth")
    own_j = lax.axis_index("map")
    me = own_i * n_map + own_j

    def place(linear):
        return (lax.div(linear, n_map), lax.rem(linear, n_map))

    links = [
        (0, 0, own_i < n_depth - 1, (own_i + 1, own_j), own_i > 0, (own_i - 1, own_j)),
        (1, 0, own_i > 0, (own_i - 1, own_j), own_i < n_depth - 1, (own_i + 1, own_j)),
        (2, 1, own_j < n_map - 1, (own_i, own_j + 1), own_j > 0, (own_i, own_j - 1)),
        (3, 1, own_j > 0, (own_i, own_j - 1), own_j < n_map - 1, (own_i, own_j + 1)),
    ]

    recv_buf[...] = jnp.zeros_like(recv_buf)
    cells_main[...] = jnp.zeros_like(cells_main)
    cells_side[...] = jnp.zeros_like(cells_side)

    barrier = pltpu.get_barrier_semaphore()
    for slot, tile, to_ok, target, from_ok, source in links:

        @pl.when(from_ok)
        def _(source=source):
            pl.semaphore_signal(barrier, inc=1, device_id=source, device_id_type=MESH)

    def main_source(j):
        return lax.div(me + n_dev * j, per_dev)

    def side_source(j):
        cell = me + n_dev * j
        place_in = lax.rem(cell, per_dev)
        home = lax.div(cell, per_dev)
        below = jnp.logical_and(place_in == 0, home > 0)
        above = jnp.logical_and(place_in == per_dev - 1, home < n_dev - 1)
        source = jnp.where(below, home - 1, home + 1)
        return jnp.logical_or(below, above), jnp.clip(source, 0, n_dev - 1)

    def greet(j, carry):
        main = main_source(j)

        @pl.when(main != me)
        def _():
            pl.semaphore_signal(barrier, inc=1, device_id=place(main), device_id_type=MESH)

        exists, side = side_source(j)

        @pl.when(jnp.logical_and(exists, side != me))
        def _():
            pl.semaphore_signal(barrier, inc=1, device_id=place(side), device_id_type=MESH)

        return carry

    lax.fori_loop(0, per_dev, greet, 0)

    three_zero = jnp.zeros((128, 256), F32)

    def three_parts(matrix, step_lanes, rows):
        square[0, 0:rows, 0:128] = matrix[0:rows]
        high, low = split(square[0, 0:rows, :])
        high, low = high.astype(F32), low.astype(F32)
        joined = high + pltpu.roll(high, step_lanes, 1) + pltpu.roll(low, 2 * step_lanes, 1)
        return joined.astype(BF16)

    square[0] = three_zero
    for d in range(3):
        square[1] = three_zero
        square[1, 0:basis, 0:basis] = stiff_ref[d]
        flipped = square[1, :, 0:128].T
        amat_ref[d * ROWS : (d + 1) * ROWS, :] = three_parts(flipped, KROWS, ROWS)
    square[1] = three_zero
    for g in range(4):
        square[1, g * 16 : g * 16 + face_ref.shape[0], 0:basis] = face_ref[:, g, :]
    tracing = square[1, :, 0:128]
    amat_ref[3 * ROWS : 3 * ROWS + 64, :] = three_parts(tracing, KROWS, 64)
    lmat_ref[...] = three_parts(tracing.T, 64, ROWS)

    p_speed, s_speed, density = p_ref[...], s_ref[...], rho_ref[...]
    lame = density * (p_speed * p_speed - 2.0 * s_speed * s_speed)
    shear = density * s_speed * s_speed
    inv_rho = 1.0 / density

    def keep(index, row):
        coef[index] = jnp.broadcast_to(row, (8, count))

    for d in range(3):
        for a in range(3):
            row = jac_ref[d, a : a + 1, :]
            keep(d * 3 + a, row)
            keep(9 + d * 3 + a, HALF * inv_rho * row)
    keep(18, HALF * lame)
    keep(19, 2.0 * HALF * shear)
    keep(20, HALF * shear)
    azimuth, polar = ang_ref[0], ang_ref[1]
    sin_polar = jnp.sin(polar)
    normal = [jnp.cos(azimuth) * sin_polar, jnp.sin(azimuth) * sin_polar, jnp.cos(polar)]
    weight = (0.5 * FULL) * scale_ref[...]
    for f in range(4):
        for a in range(3):
            keep(21 + f * 3 + a, weight[f : f + 1] * normal[a][f : f + 1])
        keep(37 + f, weight[f : f + 1] * p_speed)
    keep(33, lame)
    keep(34, 2.0 * shear)
    keep(35, shear)
    keep(36, inv_rho)

    ghosts = 256
    locals_all = 4 * count
    row_ids = lax.broadcasted_iota(jnp.int32, (256, count), 0)
    for f in range(4):
        nbr = nbr_ref[f : f + 1, :]
        local = nface_ref[f : f + 1, :] * count + nbr
        outer = jnp.where(nbr < count + ghosts, nbr - count + locals_all, -1)
        index = jnp.where(nbr < count, local, outer)
        for block in range((locals_all + ghosts) // 256):
            hit = (row_ids + block * 256) == index
            onehot[block * 256 : (block + 1) * 256, f * count : (f + 1) * count] = jnp.where(
                hit, 1.0, 0.0
            ).astype(BF16)
    send_row[...] = jnp.zeros_like(send_row)
    send_row[0:4, 0:64] = sface_ref[...] * count + send_ref[...]
    send_lane = lax.broadcasted_iota(jnp.int32, (8, 128), 1)
    shifted = pltpu.roll(send_row[...], 64, 1)
    send_ids = lax.broadcasted_iota(jnp.int32, (256, 128), 0)
    for tile in range(2):
        index = jnp.where(
            send_lane[0:1] < 64, send_row[2 * tile : 2 * tile + 1, :], shifted[2 * tile + 1 : 2 * tile + 2]
        )
        for block in range(locals_all // 256):
            hit = (send_ids + block * 256) == index
            send_hot[block * 256 : (block + 1) * 256, tile * 128 : (tile + 1) * 128] = jnp.where(
                hit, 1.0, 0.0
            ).astype(BF16)

    q_buf[:, 32:ROWS, :] = jnp.zeros((9, 8, count), F32)
    f_buf[:, 32:ROWS, :] = jnp.zeros((9, 8, count), F32)
    q_buf[:, 0:basis, :] = adj_ref[...]
    b_buf[...] = jnp.zeros_like(b_buf)
    sums[...] = jnp.zeros_like(sums)

    half = count // 2
    halves = (slice(0, half), slice(half, count))

    def load_operand(source, h):
        for field in range(9):
            high, low = split(source[field, :, halves[h]])
            b_buf[field, 0:ROWS, halves[h]] = high
            b_buf[field, KROWS : KROWS + ROWS, halves[h]] = low
            b_buf[field, 2 * KROWS : 2 * KROWS + ROWS, halves[h]] = high

    def volume(field, h, start=0, stop=3 * ROWS):
        y_buf[field, start:stop, halves[h]] = wide_dot(
            amat_ref[start:stop, 0 : 3 * KROWS], b_buf[field, :, halves[h]]
        )

    def advance(factor, h):
        for t in range(h * tiles // 2, (h + 1) * tiles // 2):
            lanes = slice(t * 128, (t + 1) * 128)
            lame_c = coef[18, :, lanes] * factor
            two_c = coef[19, :, lanes] * factor
            shear_c = coef[20, :, lanes] * factor
            for r in range(ROWS // 8):
                rows = slice(r * 8, r * 8 + 8)

                def moved(d, field):
                    return y_buf[field, d * ROWS + r * 8 : d * ROWS + r * 8 + 8, lanes]

                grad = {}
                for b in range(3):
                    parts = [moved(d, 6 + b) for d in range(3)]
                    for a in range(3):
                        grad[a, b] = (
                            coef[a, :, lanes] * parts[0]
                            + coef[3 + a, :, lanes] * parts[1]
                            + coef[6 + a, :, lanes] * parts[2]
                        )
                dil = lame_c * (grad[0, 0] + grad[1, 1] + grad[2, 2])
                for a in range(3):
                    p_buf[a, rows, lanes] = q_buf[a, rows, lanes] - dil - two_c * grad[a, a]
                for field, a, b in ((3, 0, 1), (4, 1, 2), (5, 0, 2)):
                    p_buf[field, rows, lanes] = q_buf[field, rows, lanes] - shear_c * (
                        grad[a, b] + grad[b, a]
                    )
                stress = [[moved(d, field) for d in range(3)] for field in range(6)]
                for b, picks in ((0, (0, 3, 5)), (1, (3, 1, 4)), (2, (5, 4, 2))):
                    total = None
                    for d in range(3):
                        for a in range(3):
                            term = coef[9 + d * 3 + a, :, lanes] * stress[picks[a]][d]
                            total = term if total is None else total + term
                    p_buf[6 + b, rows, lanes] = q_buf[6 + b, rows, lanes] - factor * total
                yield

    def element_sums(step):
        for field in range(9):
            f_buf[field, 0:basis, :] = fwd_ref[step, field].astype(F32)
        for t in range(tiles):
            lanes = slice(t * 128, (t + 1) * 128)
            first, second, third = None, None, None
            for r in range(ROWS // 8):
                rows = slice(r * 8, r * 8 + 8)
                x = [p_buf[field, rows, lanes] for field in range(9)]
                y = [f_buf[field, rows, lanes] for field in range(9)]
                one = (x[0] + x[1] + x[2]) * (y[0] + y[1] + y[2])
                two = (x[0] * y[0] + x[1] * y[1] + x[2] * y[2]) + 2.0 * (
                    x[3] * y[3] + x[4] * y[4] + x[5] * y[5]
                )
                three = x[6] * y[6] + x[7] * y[7] + x[8] * y[8]
                first = one if first is None else first + one
                second = two if second is None else second + two
                third = three if third is None else third + three
            sums[0, :, lanes] += first
            sums[1, :, lanes] += second
            sums[2, :, lanes] += third
            yield

    def ghost_copy(step, link):
        slot, tile, to_ok, target, from_ok, source = link
        return pltpu.make_async_remote_copy(
            src_ref=send_buf.at[step, slot],
            dst_ref=recv_buf.at[step, slot],
            send_sem=g_send.at[step, slot],
            recv_sem=g_recv.at[step, slot],
            device_id=target,
            device_id_type=MESH,
        )

    pl.semaphore_wait(
        barrier,
        sum(link[2].astype(jnp.int32) for link in links) + target_count(me, n_dev, per_dev),
    )

    def cell_copy(c, cell, dst, sem):
        target = lax.rem(cell, n_dev)
        slot = lax.div(cell, n_dev)
        return pltpu.make_async_remote_copy(
            src_ref=cells_out,
            dst_ref=dst.at[slot],
            send_sem=h_send.at[c],
            recv_sem=sem.at[slot],
            device_id=place(target),
            device_id_type=MESH,
        )

    def to_cell(c, cell, dst, sem):
        target = lax.rem(cell, n_dev)
        slot = lax.div(cell, n_dev)

        @pl.when(target != me)
        def _():
            cell_copy(c, cell, dst, sem).start()

        @pl.when(target == me)
        def _():
            dst[slot] = cells_out[...]

    low_cell = per_dev * me - 1
    high_cell = per_dev * me + per_dev

    def send_cells():
        parts = [jnp.sum(sums[k], axis=0, keepdims=True) for k in range(3)]
        first, second, third = parts
        gain = KERNEL_WEIGHT * FULL
        speed_sq = s_speed * s_speed
        terms = [
            gain * (2.0 * density * p_speed * first),
            gain * (density * s_speed * (2.0 * second - 4.0 * first)),
            gain * ((p_speed * p_speed - 2.0 * speed_sq) * first + speed_sq * second + third),
        ]
        term_row = lax.broadcasted_iota(jnp.int32, (8, count), 0)
        stacked = jnp.where(term_row == 0, terms[0], 0.0)
        stacked = jnp.where(term_row == 1, terms[1], stacked)
        stacked = jnp.where(term_row == 2, terms[2], stacked)
        entry = cell_ref[...]
        owner = lax.shift_right_logical(entry, per_dev.bit_length() - 1)
        coarse = (entry - owner * per_dev) * n_dev + owner
        relative = coarse - (per_dev * me - 1)
        hot = jnp.where(
            lax.broadcasted_iota(jnp.int32, (128, count), 0) == relative, 1.0, 0.0
        ).astype(F32)
        cells_out[...] = lax.dot_general(
            stacked,
            hot,
            (((1,), (1,)), ((), ())),
            precision=lax.Precision.HIGHEST,
            preferred_element_type=F32,
        )

        def send_main(c, carry):
            to_cell(c, per_dev * me + c, cells_main, h_recv_main)
            return carry

        lax.fori_loop(0, per_dev, send_main, 0)

        @pl.when(me > 0)
        def _():
            to_cell(per_dev, low_cell, cells_side, h_recv_side)

        @pl.when(me < n_dev - 1)
        def _():
            to_cell(per_dev + 1, high_cell, cells_side, h_recv_side)

    def step_body(step, carry):
        load_operand(q_buf, 0)
        load_operand(q_buf, 1)
        base = 3 * ROWS
        half_lane = lax.broadcasted_iota(jnp.int32, (TRACE // 2, 128), 1)
        for field in range(9):
            volume(field, 0)

        def sweep(_, inner):
            for h in range(2):
                pieces = advance(1.0, h)
                for field in range(9):
                    volume(field, 1 - h)
                    next(pieces)
                for _ in pieces:
                    pass
                load_operand(p_buf, h)
            return inner

        lax.fori_loop(0, PICARD, sweep, 0)
        for field in range(9):
            volume(field, 0, base, base + 64)
            volume(field, 1, 0, base + 64)
        for _ in element_sums(step):
            pass
        for field in range(9):
            for g in range(4):
                high, low = split(y_buf[field, base + g * 16 : base + g * 16 + 16, :])
                columns = slice(g * count, (g + 1) * count)
                left_buf[field * 16 : field * 16 + 16, columns] = high
                left_buf[TRACE + field * 16 : TRACE + field * 16 + 16, columns] = low
        picked = wide_dot(left_buf[...], send_hot[...])
        picked = picked[0:TRACE] + picked[TRACE:]
        for tile in range(2):
            block = picked[:, tile * 128 : (tile + 1) * 128]
            top, bottom = block[0 : TRACE // 2], block[TRACE // 2 :]
            turned_top, turned_bottom = pltpu.roll(top, 64, 1), pltpu.roll(bottom, 64, 1)
            send_buf[step, 2 * tile] = jnp.where(half_lane < 64, top, turned_bottom)
            send_buf[step, 2 * tile + 1] = jnp.where(half_lane < 64, turned_top, bottom)
        for link in links:

            @pl.when(link[2])
            def _(link=link):
                ghost_copy(step, link).start()

        @pl.when(step == steps - 1)
        def _():
            send_cells()

        def side_work():
            yield from advance(2.0, 0)
            yield from advance(2.0, 1)

        work = side_work()
        for c in range(8):
            columns = slice(c * half, (c + 1) * half)
            got = wide_dot(left_buf[...], onehot[0:locals_all, columns])
            far_buf[:, columns] = got[0:TRACE] + got[TRACE:]
            for _ in range(3):
                next(work, None)
        for _ in work:
            pass

        for link in links:

            @pl.when(link[4])
            def _(link=link):
                ghost_copy(step, link).wait_recv()

        for tile in range(2):
            even, odd = recv_buf[step, 2 * tile], recv_buf[step, 2 * tile + 1]
            top = jnp.where(half_lane < 64, even, pltpu.roll(odd, 64, 1))
            bottom = jnp.where(half_lane < 64, pltpu.roll(even, 64, 1), odd)
            high, low = split(jnp.concatenate([top, bottom], axis=0))
            ghost_left[0:TRACE, tile * 128 : (tile + 1) * 128] = high
            ghost_left[TRACE:, tile * 128 : (tile + 1) * 128] = low
        for f in range(4):
            columns = slice(f * count, (f + 1) * count)
            got = wide_dot(ghost_left[...], onehot[locals_all:, columns])
            far_buf[:, columns] += got[0:TRACE] + got[TRACE:]

        for f in range(4):
            for t in range(tiles):
                lanes = slice(t * 128, (t + 1) * 128)
                far_lanes = slice(f * count + t * 128, f * count + (t + 1) * 128)
                nx, ny, nz = (coef[21 + f * 3 + a, :, lanes] for a in range(3))
                lame_c, two_c = coef[33, :, lanes], coef[34, :, lanes]
                shear_c, inv_c = coef[35, :, lanes], coef[36, :, lanes]
                speed = coef[37 + f, :, lanes]
                for r in range(2):
                    own = [
                        y_buf[k, base + f * 16 + r * 8 : base + f * 16 + r * 8 + 8, lanes]
                        for k in range(9)
                    ]
                    far = [
                        far_buf[k * 16 + r * 8 : k * 16 + r * 8 + 8, far_lanes] for k in range(9)
                    ]
                    x = [own[k] + far[k] for k in range(9)]
                    jump = [speed * (own[k] - far[k]) for k in range(9)]
                    gx, gy, gz = nx * x[6], ny * x[7], nz * x[8]
                    dil = lame_c * (gx + gy + gz)
                    flux = [
                        jump[0] - dil - two_c * gx,
                        jump[1] - dil - two_c * gy,
                        jump[2] - dil - two_c * gz,
                        jump[3] - shear_c * (ny * x[6] + nx * x[7]),
                        jump[4] - shear_c * (nz * x[7] + ny * x[8]),
                        jump[5] - shear_c * (nz * x[6] + nx * x[8]),
                        jump[6] - inv_c * (nx * x[0] + ny * x[3] + nz * x[5]),
                        jump[7] - inv_c * (nx * x[3] + ny * x[1] + nz * x[4]),
                        jump[8] - inv_c * (nx * x[5] + ny * x[4] + nz * x[2]),
                    ]
                    for k in range(9):
                        flux_buf[k, f * 16 + r * 8 : f * 16 + r * 8 + 8, lanes] = flux[k]
        for field in range(9):
            high, low = split(flux_buf[field])
            fx_buf[0:64, :] = high
            fx_buf[64:128, :] = low
            fx_buf[128:192, :] = high
            q_buf[field] = p_buf[field] - wide_dot(lmat_ref[:, 0:192], fx_buf[...])
        for link in links:

            @pl.when(link[2])
            def _(link=link):
                ghost_copy(step, link).wait_send()

        return carry

    lax.fori_loop(0, steps, step_body, 0)
    out_ref[...] = q_buf[:, 0:basis, :]

    def finish(j, carry):
        @pl.when(main_source(j) != me)
        def _():
            pltpu.make_async_copy(cells_out, cells_main.at[j], h_recv_main.at[j]).wait()

        exists, side = side_source(j)

        @pl.when(jnp.logical_and(exists, side != me))
        def _():
            pltpu.make_async_copy(cells_out, cells_side.at[j], h_recv_side.at[j]).wait()

        return carry

    lax.fori_loop(0, per_dev, finish, 0)

    lane = lax.broadcasted_iota(jnp.int32, (8, 128), 1)
    inner = lax.rem(me, per_dev)
    main_lane = inner + 1
    side_lane = jnp.where(inner == 0, per_dev + 1, 0)
    result = jnp.zeros((8, 128), F32)
    for j in range(per_dev):
        value = jnp.where(lane == main_lane, cells_main[j], 0.0)
        value = value + jnp.where(lane == side_lane, cells_side[j], 0.0)
        result = jnp.where(lane == j, jnp.sum(value, axis=1, keepdims=True), result)
    hist_ref[...] = result[0:3, 0:per_dev]

    def drain(c, carry):
        @pl.when(lax.rem(per_dev * me + c, n_dev) != me)
        def _():
            pltpu.make_async_copy(cells_out, cells_main.at[0], h_send.at[c]).wait()

        return carry

    lax.fori_loop(0, per_dev, drain, 0)

    @pl.when(jnp.logical_and(me > 0, lax.rem(jnp.maximum(low_cell, 0), n_dev) != me))
    def _():
        pltpu.make_async_copy(cells_out, cells_side.at[0], h_send.at[per_dev]).wait()

    @pl.when(jnp.logical_and(me < n_dev - 1, lax.rem(high_cell, n_dev) != me))
    def _():
        pltpu.make_async_copy(cells_out, cells_side.at[0], h_send.at[per_dev + 1]).wait()


def target_count(me, n_dev, per_dev):
    total = jnp.int32(0)
    for c in range(per_dev):
        total = total + (lax.rem(per_dev * me + c, n_dev) != me).astype(jnp.int32)
    low_cell = per_dev * me - 1
    high_cell = per_dev * me + per_dev
    low = jnp.logical_and(me > 0, lax.rem(jnp.maximum(low_cell, 0), n_dev) != me)
    high = jnp.logical_and(me < n_dev - 1, lax.rem(high_cell, n_dev) != me)
    return total + low.astype(jnp.int32) + high.astype(jnp.int32)


def hand_over(state_ref, cells_ref, out_ref, hist_ref, sems):
    copies = [
        pltpu.make_async_copy(state_ref, out_ref, sems.at[0]),
        pltpu.make_async_copy(cells_ref, hist_ref, sems.at[1]),
    ]
    for copy in copies:
        copy.start()
    for copy in copies:
        copy.wait()


def shards(
    n_depth,
    n_map,
    adjoint,
    forward,
    p_speed,
    s_speed,
    density,
    inv_jacobian,
    face_angles,
    face_scale,
    stiffness,
    face_basis,
    neighbours,
    neighbour_face,
    send_elements,
    send_faces,
    cell_index,
):
    basis, fields, count = adjoint.shape
    steps = forward.shape[0]
    per_dev = count // 32
    row = lambda value: value.reshape(1, count)
    vmem = pl.BlockSpec(memory_space=pltpu.VMEM)
    anywhere = pl.BlockSpec(memory_space=pl.ANY)
    state, kernels = pl.pallas_call(
        functools.partial(kernel, n_depth, n_map),
        out_shape=(
            jax.ShapeDtypeStruct((fields, basis, count), F32),
            jax.ShapeDtypeStruct((3, per_dev), F32),
        ),
        in_specs=[vmem] * 15,
        out_specs=(vmem, vmem),
        scratch_shapes=[
            pltpu.VMEM((3 * ROWS + 64, 256), BF16),
            pltpu.VMEM((ROWS, 256), BF16),
            pltpu.VMEM((2, 128, 256), F32),
            pltpu.VMEM((8, 128), jnp.int32),
            pltpu.VMEM((9, ROWS, count), F32),
            pltpu.VMEM((9, ROWS, count), F32),
            pltpu.VMEM((9, 3 * KROWS, count), BF16),
            pltpu.VMEM((9, 3 * ROWS + 64, count), F32),
            pltpu.VMEM((9, ROWS, count), F32),
            pltpu.VMEM((41, 8, count), F32),
            pltpu.VMEM((4 * count + 256, 4 * count), BF16),
            pltpu.VMEM((4 * count, 256), BF16),
            pltpu.VMEM((2 * TRACE, 4 * count), BF16),
            pltpu.VMEM((2 * TRACE, 256), BF16),
            pltpu.VMEM((TRACE, 4 * count), F32),
            pltpu.VMEM((9, 64, count), F32),
            pltpu.VMEM((192, count), BF16),
            pltpu.VMEM((3, 8, count), F32),
            pltpu.VMEM((steps, 4, TRACE // 2, 128), F32),
            pltpu.VMEM((steps, 4, TRACE // 2, 128), F32),
            pltpu.VMEM((8, 128), F32),
            pltpu.VMEM((per_dev, 8, 128), F32),
            pltpu.VMEM((per_dev, 8, 128), F32),
            pltpu.SemaphoreType.DMA((steps, 4)),
            pltpu.SemaphoreType.DMA((steps, 4)),
            pltpu.SemaphoreType.DMA((per_dev + 2,)),
            pltpu.SemaphoreType.DMA((per_dev,)),
            pltpu.SemaphoreType.DMA((per_dev,)),
        ],
        compiler_params=pltpu.CompilerParams(
            collective_id=0, has_side_effects=True, vmem_limit_bytes=36 * 1024 * 1024
        ),
    )(
        jnp.transpose(adjoint, (1, 0, 2)),
        jnp.transpose(forward, (0, 2, 1, 3)),
        row(p_speed),
        row(s_speed),
        row(density),
        inv_jacobian,
        face_angles,
        face_scale,
        stiffness,
        jnp.transpose(face_basis, (2, 0, 1)),
        neighbours,
        neighbour_face,
        send_elements,
        send_faces,
        row(cell_index),
    )
    state, kernels = pl.pallas_call(
        hand_over,
        out_shape=(
            jax.ShapeDtypeStruct(state.shape, F32),
            jax.ShapeDtypeStruct(kernels.shape, F32),
        ),
        in_specs=[anywhere] * 2,
        out_specs=(anywhere, anywhere),
        scratch_shapes=[pltpu.SemaphoreType.DMA((2,))],
        compiler_params=pltpu.CompilerParams(vmem_limit_bytes=1024 * 1024),
    )(state, kernels)
    return jnp.transpose(state, (1, 0, 2)), kernels


def solution(mesh):
    n_depth, n_map = mesh.shape["depth"], mesh.shape["map"]
    both = ("depth", "map")
    placed = (
        P(None, None, both),
        P(None, None, None, both),
        P(both),
        P(both),
        P(both),
        P(None, None, both),
        P(None, None, both),
        P(None, both),
        P(),
        P(),
        P(None, both),
        P(None, both),
        P(None, both),
        P(None, both),
        P(both),
    )
    return jax.shard_map(
        functools.partial(shards, n_depth, n_map),
        mesh=mesh,
        in_specs=placed,
        out_specs=(P(None, None, both), P(None, both)),
        check_vma=False,
    )
```
